32 devices in a mesh: seq: 8 (over z, y), batch: 4 (over x, core).
Axes of the slice: x: 2, y: 2, z: 4, core: 2. Of those that a mesh axis runs over, the one named last changes fastest.
Arguments:
- queries: bfloat16 [8192, 256], P(('batch', 'seq')), parts along dimension 0, may hold values from -0.5 to 0.5
- keys: bfloat16 [8192, 256], P(('batch', 'seq')), parts along dimension 0, may hold values from -0.5 to 0.5
- values: bfloat16 [8192, 512], P(('batch', 'seq')), parts along dimension 0, may hold values from -6 to 6
- log_decay: float32 [8192, 256], P(('batch', 'seq')), parts along dimension 0, may hold values from -1 to 0, as said below
- out_grad: bfloat16 [8192, 512], P(('batch', 'seq')), parts along dimension 0, may hold values from -0.19921875 to 0.19921875
Outputs:
- grad_queries: bfloat16 [8192, 256], P(('batch', 'seq')), parts along dimension 0
- grad_keys: bfloat16 [8192, 256], P(('batch', 'seq')), parts along dimension 0
- grad_values: bfloat16 [8192, 512], P(('batch', 'seq')), parts along dimension 0
- grad_decay: float32 [8192, 256], P(('batch', 'seq')), parts along dimension 0
The draws below stay inside these ranges and needn't reach their ends.
There are 4 independent parts, one for each index of `batch`. The reference program is written for one: setup_inputs(seed, part) draws one part's arguments, and reference() takes and returns one part's arrays. A program takes and returns all parts, laid end to end along the dimension named above; each array names one. Nothing has to cross between parts.
Inputs may be any that keep to these rules, and one draw needn't show every extreme that they name: `log_decay`: log of a decay factor per position and key channel.
All inputs are finite; a program needn't handle non-finite values.
Results may differ from the reference program's by a relative error of at most 0.001.
Values sent between devices are 32-bit elements; how exact they have to be, the bound alone decides.
A program may use at most 128 MiB of HBM per device.

```python
import jax
import jax.numpy as jnp
from jax import lax

H = 2
K = 128
V = 256
GROUP = 64
TOK_DEV = 256
LENGTH = 2048
N_SEQ = 8


def draw_log_decay(key, part):
    sequence_extent = TOK_DEV * N_SEQ
    hidden_dimension = H * K
    number_of_streams = jax.random.split(jax.random.fold_in(key, 17), 7)
    fast_share = 0.5
    fast = jax.random.bernoulli(number_of_streams[0], fast_share, (hidden_dimension,))
    span = jax.random.uniform(number_of_streams[1], (hidden_dimension,), jnp.float32, 30.0, 50.0)
    slow_scale = jax.random.uniform(number_of_streams[2], (hidden_dimension,), jnp.float32, 0.03, 0.15)
    base = jnp.where(fast, jnp.log(10.0) / span, slow_scale * jnp.log(10.0) / sequence_extent)
    device_factor = jnp.exp(jax.random.uniform(number_of_streams[3], (N_SEQ, 1, hidden_dimension), jnp.float32, -0.69, 0.69))
    rough = jax.random.uniform(number_of_streams[4], (N_SEQ, TOK_DEV, hidden_dimension), jnp.float32, 0.5, 1.5)
    incoming_frequency = (base[None, None, :] * device_factor * rough).reshape(sequence_extent, hidden_dimension)
    places = jax.random.randint(number_of_streams[5], (2,), 0, sequence_extent)
    number_of_hits = jnp.any(jnp.arange(sequence_extent)[:, None] == places[None, :], axis=1)
    packet_quantity = jnp.log(jax.random.uniform(number_of_streams[6], (sequence_extent, hidden_dimension), jnp.float32, 0.5, 0.8))
    return (-incoming_frequency + jnp.where(number_of_hits[:, None], packet_quantity, 0.0)).astype(jnp.float32)


def levels(stream_key, extent, shards, low, largest):
    factor_of, own = 1.0, jax.random.fold_in(stream_key, 6)
    for position, blocks in shards:
        draws = jnp.exp(jax.random.uniform(jax.random.fold_in(own, position), (blocks,), jnp.float32, low / len(shards), largest / len(shards)))
        factor_of = factor_of * jnp.repeat(draws, extent[position] // blocks).reshape([-1 if axis == position else 1 for axis in range(len(extent))])
    return factor_of


def normal_values(key, dims, spread, bound, cuts=(), held_as=jnp.bfloat16):
    level = levels(key, dims, cuts, -0.22, 0.18) if cuts else 1.0
    result = jax.random.normal(key, dims, jnp.float32) * spread * level
    return jnp.minimum(jnp.maximum(result, -bound), bound).astype(held_as)


def setup_inputs(seed: int = 0, part: int = 0) -> dict:
    key_of = jax.random.split(jax.random.key(seed), 6)
    part_splits = jax.random.split(jax.random.fold_in(key_of[5], part), 6)
    queries = normal_values(part_splits[0], (LENGTH, H * K), K ** -0.5, 0.5, ((0, 8),))
    keys = normal_values(part_splits[1], (LENGTH, H * K), K ** -0.5, 0.5, ((0, 8),))
    values = normal_values(part_splits[2], (LENGTH, H * V), 1.0, 6.0, ((0, 8),))
    log_decay = draw_log_decay(jax.random.fold_in(jax.random.fold_in(key_of[5], part), 71), part)
    out_grad = normal_values(part_splits[4], (LENGTH, H * V), 0.03125, 0.19921875, ((0, 8),))
    return dict(queries=queries, keys=keys, values=values, log_decay=log_decay, out_grad=out_grad)


HIGHEST_PRECISION = lax.Precision.HIGHEST


def outer_product(form, left, right):
    return jnp.einsum(form, left, right, precision=HIGHEST_PRECISION, preferred_element_type=jnp.float32)


def reference(queries, keys, values, log_decay, out_grad):
    sequence_extent = queries.shape[0]
    blocks = sequence_extent // GROUP
    query_rows = queries.astype(jnp.float32).reshape(blocks, GROUP, H, K)
    key_rows = keys.astype(jnp.float32).reshape(blocks, GROUP, H, K)
    value_rows = values.astype(jnp.float32).reshape(blocks, GROUP, H, V)
    grad_rows = out_grad.astype(jnp.float32).reshape(blocks, GROUP, H, V)
    within = jnp.cumsum(log_decay.reshape(blocks, GROUP, H, K), axis=1)
    block_sum = within[:, -1]
    rising = jnp.exp(within)
    falling = jnp.exp(-within)
    tail_gate = jnp.exp(block_sum[:, None] - within)
    q_gate = query_rows * rising
    k_gate = key_rows * falling
    k_tail = key_rows * tail_gate
    causal = jnp.tril(jnp.ones((GROUP, GROUP), jnp.float32))
    zero_state = jnp.zeros((H, K, V), jnp.float32)

    def forward_step(carried_state, inputs):
        kg_block, lookup_final_slab, value_tile, gradient_tile, rise_block, summed_decay = inputs
        pair_dots = outer_product('thv,shv->hts', gradient_tile, value_tile) * causal
        grad_q = rise_block * (outer_product('hts,shk->thk', pair_dots, kg_block)
                               + outer_product('pzn,zyn->pzy', gradient_tile, carried_state))
        carried_state = jnp.exp(summed_decay)[..., None] * carried_state + outer_product('mln,mls->lns', lookup_final_slab, value_tile)
        return carried_state, grad_q

    unused_end, grad_q = lax.scan(forward_step, zero_state,
                                  (k_gate, k_tail, value_rows, grad_rows, rising, block_sum))

    def backward_step(carried_gradient, inputs):
        query_gate_tile, kg_block, lookup_final_slab, value_tile, gradient_tile, fall_block, trailing_tile, summed_decay = inputs
        score_matrix = outer_product('thk,shk->hts', query_gate_tile, kg_block) * causal
        pair_dots = outer_product('thv,shv->hts', gradient_tile, value_tile) * causal
        grad_k = fall_block * outer_product('hts,thk->shk', pair_dots, query_gate_tile) \
            + trailing_tile * outer_product('bdz,dlz->bdl', value_tile, carried_gradient)
        value_gradient = outer_product('nbj,bne->jne', score_matrix, gradient_tile) + outer_product('icd,cda->ica', lookup_final_slab, carried_gradient)
        carried_gradient = outer_product('mln,mls->lns', query_gate_tile, gradient_tile) + jnp.exp(summed_decay)[..., None] * carried_gradient
        return carried_gradient, (grad_k, value_gradient)

    unused_start, (grad_k, value_gradient) = lax.scan(
        backward_step, zero_state,
        (q_gate, k_gate, k_tail, value_rows, grad_rows, falling, tail_gate, block_sum), reverse=True)
    dg_terms = (query_rows * grad_q - key_rows * grad_k).reshape(sequence_extent, H * K)
    grad_decay = lax.cumsum(dg_terms, axis=0, reverse=True)
    return (grad_q.reshape(sequence_extent, H * K).astype(jnp.bfloat16),
            grad_k.reshape(sequence_extent, H * K).astype(jnp.bfloat16),
            value_gradient.reshape(sequence_extent, H * V).astype(jnp.bfloat16),
            grad_decay)
```

```python
import functools

import jax
import jax.numpy as jnp
from jax import lax
from jax.experimental import pallas as pl
from jax.experimental.pallas import tpu as pltpu
from jax.sharding import PartitionSpec as P

H = 2
GROUP = 64
ROWS = 64

F32 = jnp.float32
BF16 = jnp.bfloat16


def split(x):
    hi = x.astype(BF16)
    return hi, (x - hi.astype(F32)).astype(BF16)


def mm(a, b):
    return lax.dot_general(a, b, (((1,), (0,)), ((), ())), preferred_element_type=F32)


def mm_nt(a, b):
    return lax.dot_general(a, b, (((1,), (1,)), ((), ())), preferred_element_type=F32)


def mm_tn(a, b):
    return lax.dot_general(a, b, (((0,), (0,)), ((), ())), preferred_element_type=F32)


def three(dot, a, b):
    return dot(a[0], b[0]) + dot(a[0], b[1]) + dot(a[1], b[0])


def kernel(n_seq, L, K, V,
           q_hbm, k_hbm, v_hbm, ld_hbm, do_hbm,
           dq_hbm, dk_hbm, dv_hbm, gd_hbm,
           q_ref, k_ref, v_ref, ld_ref, do_ref,
           dq_ref, dk_ref, dv_ref, gd_ref,
           acc_q, acc_k, acc_v, rise_ref, tail_ref, whole_rise, whole_tail, kt_ref, qg_ref,
           loc, px, carry, total, ent, ec_own, ec_par,
           in_sem, out_sem, ec_sem, px_send, px_recv, near_send, near_recv, far_send, far_recv):
    blocks = L // GROUP
    per_head = V // ROWS
    chunks = H * per_head
    me = lax.axis_index("seq")
    odd = lax.rem(me, 2)
    mine = 1 - odd
    other = odd
    sign = 2 * odd - 1
    partner = me - sign
    near = me + sign
    far = me + 2 * sign
    back = me - 2 * sign
    has_dst = jnp.logical_and(far >= 0, far < n_seq)
    has_src = jnp.logical_and(back >= 0, back < n_seq)
    peers = 1 + 2 * has_dst.astype(jnp.int32) + has_src.astype(jnp.int32)
    barrier = pltpu.get_barrier_semaphore()

    loads = [
        pltpu.make_async_copy(src, dst, in_sem.at[i])
        for i, (src, dst) in enumerate(
            ((ld_hbm, ld_ref), (k_hbm, k_ref), (v_hbm, v_ref), (q_hbm, q_ref), (do_hbm, do_ref))
        )
    ]
    for copy in loads:
        copy.start()

    def tell(device):
        pl.semaphore_signal(barrier, inc=1, device_id={"seq": device},
                            device_id_type=pl.DeviceIdType.MESH)

    tell(partner)

    @pl.when(has_dst)
    def _():
        tell(near)
        tell(far)

    @pl.when(has_src)
    def _():
        tell(back)

    loads[0].wait()
    row = lax.broadcasted_iota(jnp.int32, (L, L), 0)
    col = lax.broadcasted_iota(jnp.int32, (L, L), 1)
    within = jnp.logical_and(row >= col, row // GROUP == col // GROUP)
    tri = jnp.where(within, 1.0, 0.0).astype(BF16)
    ld = ld_ref[...]
    ld0, rest = split(ld)
    mid = ld - ld0.astype(F32)
    low = (mid - rest.astype(F32)).astype(BF16)
    b = mm(tri, ld0) + mm(tri, rest) + mm(tri, low)

    def rows(n):
        return slice(n * GROUP, (n + 1) * GROUP)

    def cols(h):
        return slice(h * K, (h + 1) * K)

    def vcols(h):
        return slice(h * V, (h + 1) * V)

    c = [b[(n + 1) * GROUP - 1:(n + 1) * GROUP, :] for n in range(blocks)]
    before = [jnp.zeros_like(c[0])]
    for n in range(blocks):
        before.append(before[-1] + c[n])
    after = [jnp.zeros_like(c[0])]
    for n in reversed(range(blocks)):
        after.insert(0, after[0] + c[n])
    for n in range(blocks):
        bn = b[rows(n), :]
        rise = jnp.exp(bn)
        tail = jnp.exp(c[n] - bn)
        rise_ref[rows(n), :] = rise
        tail_ref[rows(n), :] = tail
        whole_rise[rows(n), :] = rise * jnp.exp(before[n])
        whole_tail[rows(n), :] = tail * jnp.exp(after[n + 1])
    gone = jnp.exp(before[blocks])
    for h in range(H):
        ec_own[h] = jnp.broadcast_to(gone[:, cols(h)], (8, K))

    def send(src, dst, ssem, rsem, device):
        return pltpu.make_async_remote_copy(
            src_ref=src, dst_ref=dst, send_sem=ssem, recv_sem=rsem,
            device_id={"seq": device}, device_id_type=pl.DeviceIdType.MESH)

    def part(i):
        return i // per_head, pl.ds((i % per_head) * ROWS, ROWS)

    def px_copy(i):
        h, r = part(i)
        return send(loc.at[other, h, r], px.at[h, r], px_send.at[i], px_recv.at[i], partner)

    def near_copy(i):
        h, r = part(i)
        return send(total.at[h, r], ent.at[mine, h, r], near_send.at[i], near_recv.at[i], near)

    def far_copy(i):
        h, r = part(i)
        return send(total.at[h, r], carry.at[h, r], far_send.at[i], far_recv.at[i], far)

    ec_copy = send(ec_own, ec_par, ec_sem.at[0], ec_sem.at[1], partner)

    for copy in loads[1:]:
        copy.wait()
    for h in range(H):
        ke = split(k_ref[:, cols(h)].astype(F32) * whole_tail[:, cols(h)])
        kt_ref[0, :, cols(h)] = ke[0]
        kt_ref[1, :, cols(h)] = ke[1]
        e = mm_tn(v_ref[:, vcols(h)], jnp.concatenate(ke, axis=1))
        loc[0, h] = e[:, :K] + e[:, K:]
        qf = split(q_ref[:, cols(h)].astype(F32) * whole_rise[:, cols(h)])
        f = mm_tn(do_ref[:, vcols(h)], jnp.concatenate(qf, axis=1))
        loc[1, h] = f[:, :K] + f[:, K:]
        if h == 0:
            pl.semaphore_wait(barrier, peers)
            ec_copy.start()
        for i in range(h * per_head, (h + 1) * per_head):
            px_copy(i).start()

    for h in range(H):
        k = k_ref[:, cols(h)].astype(F32)
        q = q_ref[:, cols(h)].astype(F32)
        v = v_ref[:, vcols(h)]
        do = do_ref[:, vcols(h)]
        rise = rise_ref[:, cols(h)]
        tail = tail_ref[:, cols(h)]
        bh = b[:, cols(h)]
        k_tail = k * tail
        q_gate = q * rise
        for n in range(blocks):
            width = (n + 1) * GROUP
            keys = [k_tail[rows(m), :] * jnp.exp(sum((c[j][:, cols(h)] for j in range(m + 1, n)),
                                                     jnp.zeros((1, K), F32)))
                    for m in range(n)]
            keys.append(k[rows(n), :] * jnp.exp(-bh[rows(n), :]))
            keys = split(jnp.concatenate(keys, axis=0))
            dots = mm_nt(do[rows(n), :], v[:width, :])
            t = lax.broadcasted_iota(jnp.int32, (GROUP, width), 0) + n * GROUP
            s = lax.broadcasted_iota(jnp.int32, (GROUP, width), 1)
            dots = split(jnp.where(s <= t, dots, 0.0))
            acc_q[rows(n), cols(h)] = rise[rows(n), :] * three(mm, dots, keys)

            length = L - n * GROUP
            tops = [q[rows(n), :] * jnp.exp(bh[rows(n), :] - c[n][:, cols(h)])]
            tops += [q_gate[rows(m), :] * jnp.exp(sum((c[j][:, cols(h)] for j in range(n + 1, m)),
                                                      jnp.zeros((1, K), F32)))
                     for m in range(n + 1, blocks)]
            tops = split(jnp.concatenate(tops, axis=0))
            s = lax.broadcasted_iota(jnp.int32, (GROUP, length), 0)
            t = lax.broadcasted_iota(jnp.int32, (GROUP, length), 1)
            causal = s <= t
            dots = mm_nt(v[rows(n), :], do[n * GROUP:, :])
            dots = split(jnp.where(causal, dots, 0.0))
            acc_k[rows(n), cols(h)] = tail[rows(n), :] * three(mm, dots, tops)
            scores = three(mm_nt, split(k_tail[rows(n), :]), tops)
            scores = split(jnp.where(causal, scores, 0.0))
            acc_v[rows(n), vcols(h)] = mm(scores[0], do[n * GROUP:, :]) + mm(scores[1], do[n * GROUP:, :])

    ec_copy.wait_recv()
    for i in range(chunks):
        h, r = part(i)
        px_copy(i).wait_recv()

        @pl.when(has_src)
        def _():
            far_copy(i).wait_recv()
            ent[mine, h, r] = px[h, r] + ec_par[h, 0:1, :] * carry[h, r]

        @pl.when(jnp.logical_not(has_src))
        def _():
            ent[mine, h, r] = px[h, r]

        @pl.when(has_dst)
        def _():
            total[h, r] = loc[mine, h, r] + ec_own[h, 0:1, :] * ent[mine, h, r]
            far_copy(i).start()
            near_copy(i).start()

    @pl.when(jnp.logical_not(has_dst))
    def _():
        ent[other] = jnp.zeros((H, V, K), F32)

    upper = jnp.where(row <= col, 1.0, 0.0).astype(BF16)
    stores = []
    for h in range(H):
        @pl.when(has_dst)
        def _():
            for i in range(h * per_head, (h + 1) * per_head):
                hh, r = part(i)
                send(total.at[hh, r], ent.at[other, hh, r], near_send.at[i], near_recv.at[i],
                     near).wait_recv()

        start = ent[0, h]
        end = ent[1, h]
        start2 = split(start)
        end2 = split(end)
        a = mm(do_ref[:, vcols(h)], jnp.concatenate(start2, axis=1))
        dq = acc_q[:, cols(h)] + whole_rise[:, cols(h)] * (a[:, :K] + a[:, K:])
        a = mm(v_ref[:, vcols(h)], jnp.concatenate(end2, axis=1))
        dk = acc_k[:, cols(h)] + whole_tail[:, cols(h)] * (a[:, :K] + a[:, K:])
        ke = (kt_ref[0, :, cols(h)], kt_ref[1, :, cols(h)])
        dv = acc_v[:, vcols(h)] + three(mm_nt, ke, end2)
        dq_ref[:, cols(h)] = dq.astype(BF16)
        dk_ref[:, cols(h)] = dk.astype(BF16)
        dv_ref[:, vcols(h)] = dv.astype(BF16)
        leave = ec_own[h, 0:1, :] * start + loc[0, h]
        later = jnp.sum(leave * end, axis=0, keepdims=True)
        terms = split(q_ref[:, cols(h)].astype(F32) * dq - k_ref[:, cols(h)].astype(F32) * dk)
        a = mm(upper, jnp.concatenate(terms, axis=1))
        gd_ref[:, cols(h)] = a[:, :K] + a[:, K:] + later
        for j, (src, dst, cc) in enumerate(((dq_ref, dq_hbm, cols(h)), (dk_ref, dk_hbm, cols(h)),
                                            (dv_ref, dv_hbm, vcols(h)), (gd_ref, gd_hbm, cols(h)))):
            copy = pltpu.make_async_copy(src.at[:, cc], dst.at[:, cc], out_sem.at[4 * h + j])
            copy.start()
            stores.append(copy)

    ec_copy.wait_send()
    for i in range(chunks):
        px_copy(i).wait_send()

    @pl.when(has_dst)
    def _():
        for i in range(chunks):
            far_copy(i).wait_send()
            near_copy(i).wait_send()

    for copy in stores:
        copy.wait()


def local(n_seq, queries, keys, values, log_decay, out_grad):
    L, HK = queries.shape
    HV = values.shape[1]
    K, V = HK // H, HV // H
    chunks = H * (V // ROWS)
    dma = pltpu.SemaphoreType.DMA
    any_spec = pl.BlockSpec(memory_space=pl.ANY)
    return pl.pallas_call(
        functools.partial(kernel, n_seq, L, K, V),
        out_shape=(
            jax.ShapeDtypeStruct((L, HK), BF16),
            jax.ShapeDtypeStruct((L, HK), BF16),
            jax.ShapeDtypeStruct((L, HV), BF16),
            jax.ShapeDtypeStruct((L, HK), F32),
        ),
        in_specs=[any_spec] * 5,
        out_specs=(any_spec,) * 4,
        scratch_shapes=[
            pltpu.VMEM((L, HK), BF16), pltpu.VMEM((L, HK), BF16), pltpu.VMEM((L, HV), BF16),
            pltpu.VMEM((L, HK), F32), pltpu.VMEM((L, HV), BF16),
            pltpu.VMEM((L, HK), BF16), pltpu.VMEM((L, HK), BF16), pltpu.VMEM((L, HV), BF16),
            pltpu.VMEM((L, HK), F32),
            pltpu.VMEM((L, HK), F32), pltpu.VMEM((L, HK), F32), pltpu.VMEM((L, HV), F32),
            pltpu.VMEM((L, HK), F32), pltpu.VMEM((L, HK), F32),
            pltpu.VMEM((L, HK), F32), pltpu.VMEM((L, HK), F32),
            pltpu.VMEM((2, L, HK), BF16), pltpu.VMEM((8, 128), F32),
            pltpu.VMEM((2, H, V, K), F32), pltpu.VMEM((H, V, K), F32), pltpu.VMEM((H, V, K), F32),
            pltpu.VMEM((H, V, K), F32), pltpu.VMEM((2, H, V, K), F32),
            pltpu.VMEM((H, 8, K), F32), pltpu.VMEM((H, 8, K), F32),
            dma((5,)), dma((8,)), dma((2,)), dma((chunks,)), dma((chunks,)), dma((chunks,)),
            dma((chunks,)), dma((chunks,)), dma((chunks,)),
        ],
        compiler_params=pltpu.CompilerParams(collective_id=0, has_side_effects=True),
    )(queries, keys, values, log_decay, out_grad)


def solution(mesh):
    n_seq = mesh.shape["seq"]
    spec = P(("batch", "seq"), None)
    return jax.shard_map(
        functools.partial(local, n_seq),
        mesh=mesh,
        in_specs=(spec,) * 5,
        out_specs=(spec,) * 4,
        check_vma=False,
    )
```

```python
import functools

import jax
import jax.numpy as jnp
from jax import lax
from jax.experimental import pallas as pl
from jax.experimental.pallas import tpu as pltpu
from jax.sharding import PartitionSpec as P

H = 2
GROUP = 64
ROWS = 64

F32 = jnp.float32
BF16 = jnp.bfloat16


def split(x):
    hi = x.astype(BF16)
    return hi, (x - hi.astype(F32)).astype(BF16)


def mm(a, b):
    return lax.dot_general(a, b, (((1,), (0,)), ((), ())), preferred_element_type=F32)


def mm_nt(a, b):
    return lax.dot_general(a, b, (((1,), (1,)), ((), ())), preferred_element_type=F32)


def mm_tn(a, b):
    return lax.dot_general(a, b, (((0,), (0,)), ((), ())), preferred_element_type=F32)


def three(dot, a, b):
    return dot(a[0], b[0]) + dot(a[0], b[1]) + dot(a[1], b[0])


def kernel(n_seq, L, K, V,
           q_hbm, k_hbm, v_hbm, ld_hbm, do_hbm,
           dq_ref, dk_ref, dv_ref, gd_ref,
           q_ref, k_ref, v_ref, ld_ref, do_ref,
           acc_q, acc_k, acc_v, rise_ref, tail_ref, whole_rise, whole_tail, kt_ref,
           loc, px, carry, total, ent, ec_own, ec_par,
           in_sem, ec_sem, px_send, px_recv, near_send, near_recv, far_send, far_recv):
    blocks = L // GROUP
    per_head = V // ROWS
    chunks = H * per_head
    me = lax.axis_index("seq")
    odd = lax.rem(me, 2)
    mine = 1 - odd
    other = odd
    sign = 2 * odd - 1
    partner = me - sign
    near = me + sign
    far = me + 2 * sign
    back = me - 2 * sign
    has_dst = jnp.logical_and(far >= 0, far < n_seq)
    has_src = jnp.logical_and(back >= 0, back < n_seq)
    peers = 1 + has_dst.astype(jnp.int32) + has_src.astype(jnp.int32)
    barrier = pltpu.get_barrier_semaphore()

    loads = [
        pltpu.make_async_copy(src, dst, in_sem.at[i])
        for i, (src, dst) in enumerate(
            ((ld_hbm, ld_ref), (k_hbm, k_ref), (v_hbm, v_ref), (q_hbm, q_ref), (do_hbm, do_ref))
        )
    ]
    for copy in loads:
        copy.start()

    def tell(device):
        pl.semaphore_signal(barrier, inc=1, device_id={"seq": device},
                            device_id_type=pl.DeviceIdType.MESH)

    tell(partner)

    @pl.when(has_dst)
    def _():
        tell(far)

    @pl.when(has_src)
    def _():
        tell(back)

    loads[0].wait()
    row = lax.broadcasted_iota(jnp.int32, (L, L), 0)
    col = lax.broadcasted_iota(jnp.int32, (L, L), 1)
    within = jnp.logical_and(row >= col, row // GROUP == col // GROUP)
    tri = jnp.where(within, 1.0, 0.0).astype(BF16)
    ld = ld_ref[...]
    ld0, rest = split(ld)
    mid = ld - ld0.astype(F32)
    low = (mid - rest.astype(F32)).astype(BF16)
    b = mm(tri, ld0) + mm(tri, rest) + mm(tri, low)

    def rows(n):
        return slice(n * GROUP, (n + 1) * GROUP)

    def cols(h):
        return slice(h * K, (h + 1) * K)

    def vcols(h):
        return slice(h * V, (h + 1) * V)

    c = [b[(n + 1) * GROUP - 1:(n + 1) * GROUP, :] for n in range(blocks)]
    before = [jnp.zeros_like(c[0])]
    for n in range(blocks):
        before.append(before[-1] + c[n])
    after = [jnp.zeros_like(c[0])]
    for n in reversed(range(blocks)):
        after.insert(0, after[0] + c[n])
    for n in range(blocks):
        bn = b[rows(n), :]
        rise = jnp.exp(bn)
        tail = jnp.exp(c[n] - bn)
        rise_ref[rows(n), :] = rise
        tail_ref[rows(n), :] = tail
        whole_rise[rows(n), :] = rise * jnp.exp(before[n])
        whole_tail[rows(n), :] = tail * jnp.exp(after[n + 1])
    gone = jnp.exp(before[blocks])
    for h in range(H):
        ec_own[h] = jnp.broadcast_to(gone[:, cols(h)], (8, K))

    def send(src, dst, ssem, rsem, device):
        return pltpu.make_async_remote_copy(
            src_ref=src, dst_ref=dst, send_sem=ssem, recv_sem=rsem,
            device_id={"seq": device}, device_id_type=pl.DeviceIdType.MESH)

    def part(i):
        return i // per_head, pl.ds((i % per_head) * ROWS, ROWS)

    def px_copy(i):
        h, r = part(i)
        return send(loc.at[other, h, r], px.at[h, r], px_send.at[i], px_recv.at[i], partner)

    def near_copy(i):
        h, r = part(i)
        return send(carry.at[h, r], ent.at[mine, h, r], near_send.at[i], near_recv.at[i], partner)

    def far_copy(i):
        h, r = part(i)
        return send(total.at[h, r], carry.at[h, r], far_send.at[i], far_recv.at[i], far)

    ec_copy = send(ec_own, ec_par, ec_sem.at[0], ec_sem.at[1], partner)

    for copy in loads[1:]:
        copy.wait()
    for h in range(H):
        ke = split(k_ref[:, cols(h)].astype(F32) * whole_tail[:, cols(h)])
        kt_ref[0, :, cols(h)] = ke[0]
        kt_ref[1, :, cols(h)] = ke[1]
        e = mm_tn(v_ref[:, vcols(h)], jnp.concatenate(ke, axis=1))
        loc[0, h] = e[:, :K] + e[:, K:]
        qf = split(q_ref[:, cols(h)].astype(F32) * whole_rise[:, cols(h)])
        f = mm_tn(do_ref[:, vcols(h)], jnp.concatenate(qf, axis=1))
        loc[1, h] = f[:, :K] + f[:, K:]
        if h == 0:
            pl.semaphore_wait(barrier, peers)
            ec_copy.start()
        for i in range(h * per_head, (h + 1) * per_head):
            px_copy(i).start()

    @pl.when(jnp.logical_not(has_src))
    def _():
        ec_copy.wait_recv()
        for i in range(chunks):
            h, r = part(i)
            px_copy(i).wait_recv()
            ent[mine, h, r] = px[h, r]

            @pl.when(has_dst)
            def _():
                total[h, r] = loc[mine, h, r] + ec_own[h, 0:1, :] * px[h, r]
                far_copy(i).start()

    for h in range(H):
        k = k_ref[:, cols(h)].astype(F32)
        q = q_ref[:, cols(h)].astype(F32)
        v = v_ref[:, vcols(h)]
        do = do_ref[:, vcols(h)]
        rise = rise_ref[:, cols(h)]
        tail = tail_ref[:, cols(h)]
        bh = b[:, cols(h)]
        k_tail = k * tail
        q_gate = q * rise
        for n in range(blocks):
            width = (n + 1) * GROUP
            keys = [k_tail[rows(m), :] * jnp.exp(sum((c[j][:, cols(h)] for j in range(m + 1, n)),
                                                     jnp.zeros((1, K), F32)))
                    for m in range(n)]
            keys.append(k[rows(n), :] * jnp.exp(-bh[rows(n), :]))
            keys = split(jnp.concatenate(keys, axis=0))
            dots = mm_nt(do[rows(n), :], v[:width, :])
            t = lax.broadcasted_iota(jnp.int32, (GROUP, width), 0) + n * GROUP
            s = lax.broadcasted_iota(jnp.int32, (GROUP, width), 1)
            dots = split(jnp.where(s <= t, dots, 0.0))
            acc_q[rows(n), cols(h)] = rise[rows(n), :] * three(mm, dots, keys)

            length = L - n * GROUP
            tops = [q[rows(n), :] * jnp.exp(bh[rows(n), :] - c[n][:, cols(h)])]
            tops += [q_gate[rows(m), :] * jnp.exp(sum((c[j][:, cols(h)] for j in range(n + 1, m)),
                                                      jnp.zeros((1, K), F32)))
                     for m in range(n + 1, blocks)]
            tops = split(jnp.concatenate(tops, axis=0))
            s = lax.broadcasted_iota(jnp.int32, (GROUP, length), 0)
            t = lax.broadcasted_iota(jnp.int32, (GROUP, length), 1)
            causal = s <= t
            dots = mm_nt(v[rows(n), :], do[n * GROUP:, :])
            dots = split(jnp.where(causal, dots, 0.0))
            acc_k[rows(n), cols(h)] = tail[rows(n), :] * three(mm, dots, tops)
            scores = three(mm_nt, split(k_tail[rows(n), :]), tops)
            scores = split(jnp.where(causal, scores, 0.0))
            acc_v[rows(n), vcols(h)] = mm(scores[0], do[n * GROUP:, :]) + mm(scores[1], do[n * GROUP:, :])

    @pl.when(has_src)
    def _():
        ec_copy.wait_recv()
        for i in range(chunks):
            h, r = part(i)
            px_copy(i).wait_recv()
            far_copy(i).wait_recv()
            near_copy(i).start()
            start = px[h, r] + ec_par[h, 0:1, :] * carry[h, r]
            ent[mine, h, r] = start

            @pl.when(has_dst)
            def _():
                total[h, r] = loc[mine, h, r] + ec_own[h, 0:1, :] * start
                far_copy(i).start()

    @pl.when(jnp.logical_not(has_dst))
    def _():
        ent[other] = jnp.zeros((H, V, K), F32)

    upper = jnp.where(row <= col, 1.0, 0.0).astype(BF16)
    for h in range(H):
        @pl.when(has_dst)
        def _():
            for i in range(h * per_head, (h + 1) * per_head):
                hh, r = part(i)
                send(carry.at[hh, r], ent.at[other, hh, r], near_send.at[i], near_recv.at[i],
                     partner).wait_recv()

        start = ent[0, h]
        end = ent[1, h]
        start2 = split(start)
        end2 = split(end)
        a = mm(do_ref[:, vcols(h)], jnp.concatenate(start2, axis=1))
        dq = acc_q[:, cols(h)] + whole_rise[:, cols(h)] * (a[:, :K] + a[:, K:])
        a = mm(v_ref[:, vcols(h)], jnp.concatenate(end2, axis=1))
        dk = acc_k[:, cols(h)] + whole_tail[:, cols(h)] * (a[:, :K] + a[:, K:])
        ke = (kt_ref[0, :, cols(h)], kt_ref[1, :, cols(h)])
        dv = acc_v[:, vcols(h)] + three(mm_nt, ke, end2)
        dq_ref[:, cols(h)] = dq.astype(BF16)
        dk_ref[:, cols(h)] = dk.astype(BF16)
        dv_ref[:, vcols(h)] = dv.astype(BF16)
        leave = ec_own[h, 0:1, :] * start + loc[0, h]
        later = jnp.sum(leave * end, axis=0, keepdims=True)
        terms = split(q_ref[:, cols(h)].astype(F32) * dq - k_ref[:, cols(h)].astype(F32) * dk)
        a = mm(upper, jnp.concatenate(terms, axis=1))
        gd_ref[:, cols(h)] = a[:, :K] + a[:, K:] + later

    ec_copy.wait_send()
    for i in range(chunks):
        px_copy(i).wait_send()

    @pl.when(has_dst)
    def _():
        for i in range(chunks):
            far_copy(i).wait_send()

    @pl.when(has_src)
    def _():
        for i in range(chunks):
            near_copy(i).wait_send()


def store_kernel(*refs):
    sems = refs[8]
    copies = [pltpu.make_async_copy(refs[i], refs[4 + i], sems.at[i]) for i in range(4)]
    for copy in copies:
        copy.start()
    for copy in copies:
        copy.wait()


def local(n_seq, queries, keys, values, log_decay, out_grad):
    L, HK = queries.shape
    HV = values.shape[1]
    K, V = HK // H, HV // H
    chunks = H * (V // ROWS)
    dma = pltpu.SemaphoreType.DMA
    any_spec = pl.BlockSpec(memory_space=pl.ANY)
    shapes = (((L, HK), BF16), ((L, HK), BF16), ((L, HV), BF16), ((L, HK), F32))
    held = pl.pallas_call(
        functools.partial(kernel, n_seq, L, K, V),
        out_shape=tuple(pltpu.VMEM(*a) for a in shapes),
        in_specs=[any_spec] * 5,
        out_specs=(pl.BlockSpec(memory_space=pltpu.VMEM),) * 4,
        scratch_shapes=[
            pltpu.VMEM((L, HK), BF16), pltpu.VMEM((L, HK), BF16), pltpu.VMEM((L, HV), BF16),
            pltpu.VMEM((L, HK), F32), pltpu.VMEM((L, HV), BF16),
            pltpu.VMEM((L, HK), F32), pltpu.VMEM((L, HK), F32), pltpu.VMEM((L, HV), F32),
            pltpu.VMEM((L, HK), F32), pltpu.VMEM((L, HK), F32),
            pltpu.VMEM((L, HK), F32), pltpu.VMEM((L, HK), F32),
            pltpu.VMEM((2, L, HK), BF16),
            pltpu.VMEM((2, H, V, K), F32), pltpu.VMEM((H, V, K), F32), pltpu.VMEM((H, V, K), F32),
            pltpu.VMEM((H, V, K), F32), pltpu.VMEM((2, H, V, K), F32),
            pltpu.VMEM((H, 8, K), F32), pltpu.VMEM((H, 8, K), F32),
            dma((5,)), dma((2,)), dma((chunks,)), dma((chunks,)), dma((chunks,)),
            dma((chunks,)), dma((chunks,)), dma((chunks,)),
        ],
        compiler_params=pltpu.CompilerParams(collective_id=0, has_side_effects=True),
    )(queries, keys, values, log_decay, out_grad)
    return pl.pallas_call(
        store_kernel,
        out_shape=tuple(jax.ShapeDtypeStruct(*a) for a in shapes),
        in_specs=[any_spec] * 4,
        out_specs=(any_spec,) * 4,
        scratch_shapes=[dma((4,))],
        compiler_params=pltpu.CompilerParams(vmem_limit_bytes=1 << 20),
    )(*held)


def solution(mesh):
    n_seq = mesh.shape["seq"]
    spec = P(("batch", "seq"), None)
    return jax.shard_map(
        functools.partial(local, n_seq),
        mesh=mesh,
        in_specs=(spec,) * 5,
        out_specs=(spec,) * 4,
        check_vma=False,
    )
```

```python
import functools

import jax
import jax.numpy as jnp
from jax import lax
from jax.experimental import pallas as pl
from jax.experimental.pallas import tpu as pltpu
from jax.sharding import PartitionSpec as P

H = 2
GROUP = 64
ROWS = 32

F32 = jnp.float32
BF16 = jnp.bfloat16


def split(x):
    hi = x.astype(BF16)
    return hi, (x - hi.astype(F32)).astype(BF16)


def mm(a, b):
    return lax.dot_general(a, b, (((1,), (0,)), ((), ())), preferred_element_type=F32)


def mm_nt(a, b):
    return lax.dot_general(a, b, (((1,), (1,)), ((), ())), preferred_element_type=F32)


def mm_tn(a, b):
    return lax.dot_general(a, b, (((0,), (0,)), ((), ())), preferred_element_type=F32)


def three(dot, a, b):
    return dot(a[0], b[0]) + dot(a[0], b[1]) + dot(a[1], b[0])


def kernel(n_seq, L, K, V,
           q_hbm, k_hbm, v_hbm, ld_hbm, do_hbm,
           dq_ref, dk_ref, dv_ref, gd_ref,
           qk_ref, vd_ref, ld_ref,
           acc_q, acc_k, acc_v, rise_ref, tail_ref, whole,
           loc, px, carry, total, relay, ent, ec_own, ec_par,
           in_sem, ec_sem, px_send, px_recv, near_send, near_recv, far_send, far_recv):
    blocks = L // GROUP
    per_head = V // ROWS
    me = lax.axis_index("seq")
    odd = lax.rem(me, 2)
    late = (2 * me >= n_seq).astype(jnp.int32)
    partner = me + 1 - 2 * odd
    up = me + 2 < n_seq
    down = me - 2 >= 0
    sign = (2 * odd - 1, 1 - 2 * odd)
    first = lax.rem(odd + late, 2)
    barrier = pltpu.get_barrier_semaphore()

    def pick(h, x0, x1):
        return jnp.where(h == 0, x0, x1)

    def other_of(h):
        return pick(h, odd, 1 - odd)

    def sign_of(h):
        return pick(h, sign[0], sign[1])

    def reached(device):
        return jnp.logical_and(device >= 0, device < n_seq)

    def has_dst(h):
        return reached(me + 2 * sign_of(h))

    def has_src(h):
        return reached(me - 2 * sign_of(h))

    loads = [
        pltpu.make_async_copy(src, dst, in_sem.at[i])
        for i, (src, dst) in enumerate(
            ((ld_hbm, ld_ref), (k_hbm, qk_ref.at[0]), (q_hbm, qk_ref.at[1]),
             (v_hbm, vd_ref.at[0]), (do_hbm, vd_ref.at[1]))
        )
    ]
    for copy in loads:
        copy.start()

    def tell(device):
        pl.semaphore_signal(barrier, inc=1, device_id={"seq": device},
                            device_id_type=pl.DeviceIdType.MESH)

    tell(partner)

    @pl.when(up)
    def _():
        tell(me + 2)

    @pl.when(down)
    def _():
        tell(me - 2)

    loads[0].wait()
    row = lax.broadcasted_iota(jnp.int32, (L, L), 0)
    col = lax.broadcasted_iota(jnp.int32, (L, L), 1)
    within = jnp.logical_and(row >= col, row // GROUP == col // GROUP)
    tri = jnp.where(within, 1.0, 0.0).astype(BF16)
    ld = ld_ref[...]
    ld0, rest = split(ld)
    mid = ld - ld0.astype(F32)
    low = (mid - rest.astype(F32)).astype(BF16)
    b = mm(tri, ld0) + mm(tri, rest) + mm(tri, low)

    def rows(n):
        return slice(n * GROUP, (n + 1) * GROUP)

    def cols(h):
        return slice(h * K, (h + 1) * K)

    def vcols(h):
        return slice(h * V, (h + 1) * V)

    c = [b[(n + 1) * GROUP - 1:(n + 1) * GROUP, :] for n in range(blocks)]
    before = [jnp.zeros_like(c[0])]
    for n in range(blocks):
        before.append(before[-1] + c[n])
    after = [jnp.zeros_like(c[0])]
    for n in reversed(range(blocks)):
        after.insert(0, after[0] + c[n])
    for n in range(blocks):
        bn = b[rows(n), :]
        rise = jnp.exp(bn)
        tail = jnp.exp(c[n] - bn)
        rise_ref[rows(n), :] = rise
        tail_ref[rows(n), :] = tail
        whole[1, rows(n), :] = rise * jnp.exp(before[n])
        whole[0, rows(n), :] = tail * jnp.exp(after[n + 1])
    gone = jnp.exp(before[blocks])
    for h in range(H):
        ec_own[h] = jnp.broadcast_to(gone[:, cols(h)], (8, K))

    def send(src, dst, ssem, rsem, device):
        return pltpu.make_async_remote_copy(
            src_ref=src, dst_ref=dst, send_sem=ssem, recv_sem=rsem,
            device_id={"seq": device}, device_id_type=pl.DeviceIdType.MESH)

    def part(i):
        return pl.ds(i * ROWS, ROWS)

    def px_copy(h, i):
        r = part(i)
        return send(loc.at[other_of(h), h, r], px.at[h, r], px_send.at[h, i], px_recv.at[h, i], partner)

    def near_copy(h, i):
        r = part(i)
        return send(relay.at[h, r], ent.at[1 - other_of(h), h, r], near_send.at[h, i],
                    near_recv.at[h, i], partner)

    def far_copy(h, i):
        r = part(i)
        return send(total.at[h, r], carry.at[h, r], far_send.at[h, i], far_recv.at[h, i],
                    me + 2 * sign_of(h))

    ec_copy = send(ec_own, ec_par, ec_sem.at[0], ec_sem.at[1], partner)

    for copy in loads[1:]:
        copy.wait()

    def device_total(slot, h):
        kc = pl.ds(pl.multiple_of(h * K, K), K)
        vc = pl.ds(pl.multiple_of(h * V, V), V)
        x = split(qk_ref[slot, :, kc].astype(F32) * whole[slot, :, kc])
        e = mm_tn(vd_ref[slot, :, vc], jnp.concatenate(x, axis=1))
        loc[slot, h] = e[:, :K] + e[:, K:]

    device_total(other_of(first), first)
    pl.semaphore_wait(barrier, 1 + up.astype(jnp.int32) + down.astype(jnp.int32))
    for i in range(per_head):
        px_copy(first, i).start()
    ec_copy.start()
    device_total(other_of(1 - first), 1 - first)
    for i in range(per_head):
        px_copy(1 - first, i).start()
    device_total(1 - other_of(1 - first), 1 - first)
    device_total(1 - other_of(first), first)

    def chain(h, i):
        r = part(i)
        px_copy(h, i).wait_recv()

        @pl.when(has_src(h))
        def _():
            far_copy(h, i).wait_recv()

        mine = 1 - other_of(h)
        came = carry[h, r]
        got = px[h, r]
        own = loc[mine, h, r]

        @pl.when(h == 0)
        def _():
            middle = got + ec_par[h, 0:1, :] * came
            relay[h, r] = came
            ent[mine, h, r] = middle
            total[h, r] = own + ec_own[h, 0:1, :] * middle

        @pl.when(h != 0)
        def _():
            middle = own + ec_own[h, 0:1, :] * came
            relay[h, r] = middle
            ent[mine, h, r] = came
            total[h, r] = got + ec_par[h, 0:1, :] * middle

        @pl.when(has_dst(h))
        def _():
            far_copy(h, i).start()

        @pl.when(jnp.logical_or(h != 0, has_src(h)))
        def _():
            near_copy(h, i).start()

    lead = 1 - first
    for h in range(H):
        @pl.when(jnp.logical_not(has_src(h)))
        def _():
            carry[h] = jnp.zeros((V, K), F32)

    ec_copy.wait_recv()

    @pl.when(jnp.logical_not(has_src(lead)))
    def _():
        for i in range(per_head):
            chain(lead, i)

    for h in range(H):
        k = qk_ref[0, :, cols(h)].astype(F32)
        q = qk_ref[1, :, cols(h)].astype(F32)
        v = vd_ref[0, :, vcols(h)]
        do = vd_ref[1, :, vcols(h)]
        rise = rise_ref[:, cols(h)]
        tail = tail_ref[:, cols(h)]
        bh = b[:, cols(h)]
        k_tail = k * tail
        q_gate = q * rise
        for n in range(blocks):
            width = (n + 1) * GROUP
            keys = [k_tail[rows(m), :] * jnp.exp(sum((c[j][:, cols(h)] for j in range(m + 1, n)),
                                                     jnp.zeros((1, K), F32)))
                    for m in range(n)]
            keys.append(k[rows(n), :] * jnp.exp(-bh[rows(n), :]))
            keys = split(jnp.concatenate(keys, axis=0))
            dots = mm_nt(do[rows(n), :], v[:width, :])
            t = lax.broadcasted_iota(jnp.int32, (GROUP, width), 0) + n * GROUP
            s = lax.broadcasted_iota(jnp.int32, (GROUP, width), 1)
            dots = split(jnp.where(s <= t, dots, 0.0))
            acc_q[rows(n), cols(h)] = rise[rows(n), :] * three(mm, dots, keys)

            length = L - n * GROUP
            tops = [q[rows(n), :] * jnp.exp(bh[rows(n), :] - c[n][:, cols(h)])]
            tops += [q_gate[rows(m), :] * jnp.exp(sum((c[j][:, cols(h)] for j in range(n + 1, m)),
                                                      jnp.zeros((1, K), F32)))
                     for m in range(n + 1, blocks)]
            tops = split(jnp.concatenate(tops, axis=0))
            s = lax.broadcasted_iota(jnp.int32, (GROUP, length), 0)
            t = lax.broadcasted_iota(jnp.int32, (GROUP, length), 1)
            causal = s <= t
            dots = mm_nt(v[rows(n), :], do[n * GROUP:, :])
            dots = split(jnp.where(causal, dots, 0.0))
            acc_k[rows(n), cols(h)] = tail[rows(n), :] * three(mm, dots, tops)
            scores = three(mm_nt, split(k_tail[rows(n), :]), tops)
            scores = split(jnp.where(causal, scores, 0.0))
            acc_v[rows(n), vcols(h)] = mm(scores[0], do[n * GROUP:, :]) + mm(scores[1], do[n * GROUP:, :])

    lag = (5 * per_head) // 8
    for i in range(per_head + lag):
        if i < per_head:
            @pl.when(has_src(lead))
            def _():
                chain(lead, i)
        if i >= lag:
            chain(1 - lead, i - lag)

    @pl.when(jnp.logical_not(has_dst(0)))
    def _():
        ent[odd, 0] = jnp.zeros((V, K), F32)

    upper = jnp.where(row <= col, 1.0, 0.0).astype(BF16)
    for h in range(H):
        if h == 0:
            @pl.when(has_dst(0))
            def _():
                for i in range(per_head):
                    near_copy(0, i).wait_recv()
        else:
            for i in range(per_head):
                near_copy(h, i).wait_recv()

        start = ent[0, h]
        end = ent[1, h]
        start2 = split(start)
        end2 = split(end)
        a = mm(vd_ref[1, :, vcols(h)], jnp.concatenate(start2, axis=1))
        dq = acc_q[:, cols(h)] + whole[1, :, cols(h)] * (a[:, :K] + a[:, K:])
        a = mm(vd_ref[0, :, vcols(h)], jnp.concatenate(end2, axis=1))
        dk = acc_k[:, cols(h)] + whole[0, :, cols(h)] * (a[:, :K] + a[:, K:])
        ke = split(qk_ref[0, :, cols(h)].astype(F32) * whole[0, :, cols(h)])
        dv = acc_v[:, vcols(h)] + three(mm_nt, ke, end2)
        dq_ref[:, cols(h)] = dq.astype(BF16)
        dk_ref[:, cols(h)] = dk.astype(BF16)
        dv_ref[:, vcols(h)] = dv.astype(BF16)
        leave = ec_own[h, 0:1, :] * start + loc[0, h]
        later = jnp.sum(leave * end, axis=0, keepdims=True)
        terms = split(qk_ref[1, :, cols(h)].astype(F32) * dq - qk_ref[0, :, cols(h)].astype(F32) * dk)
        a = mm(upper, jnp.concatenate(terms, axis=1))
        gd_ref[:, cols(h)] = a[:, :K] + a[:, K:] + later

    ec_copy.wait_send()
    for h in range(H):
        for i in range(per_head):
            px_copy(h, i).wait_send()

        @pl.when(has_dst(h))
        def _():
            for i in range(per_head):
                far_copy(h, i).wait_send()

        if h == 0:
            @pl.when(has_src(0))
            def _():
                for i in range(per_head):
                    near_copy(0, i).wait_send()
        else:
            for i in range(per_head):
                near_copy(h, i).wait_send()


def store_kernel(*refs):
    sems = refs[8]
    copies = [pltpu.make_async_copy(refs[i], refs[4 + i], sems.at[i]) for i in range(4)]
    for copy in copies:
        copy.start()
    for copy in copies:
        copy.wait()


def local(n_seq, queries, keys, values, log_decay, out_grad):
    L, HK = queries.shape
    HV = values.shape[1]
    K, V = HK // H, HV // H
    chunks = V // ROWS
    dma = pltpu.SemaphoreType.DMA
    any_spec = pl.BlockSpec(memory_space=pl.ANY)
    shapes = (((L, HK), BF16), ((L, HK), BF16), ((L, HV), BF16), ((L, HK), F32))
    held = pl.pallas_call(
        functools.partial(kernel, n_seq, L, K, V),
        out_shape=tuple(pltpu.VMEM(*a) for a in shapes),
        in_specs=[any_spec] * 5,
        out_specs=(pl.BlockSpec(memory_space=pltpu.VMEM),) * 4,
        scratch_shapes=[
            pltpu.VMEM((2, L, HK), BF16), pltpu.VMEM((2, L, HV), BF16), pltpu.VMEM((L, HK), F32),
            pltpu.VMEM((L, HK), F32), pltpu.VMEM((L, HK), F32), pltpu.VMEM((L, HV), F32),
            pltpu.VMEM((L, HK), F32), pltpu.VMEM((L, HK), F32), pltpu.VMEM((2, L, HK), F32),
            pltpu.VMEM((2, H, V, K), F32), pltpu.VMEM((H, V, K), F32), pltpu.VMEM((H, V, K), F32),
            pltpu.VMEM((H, V, K), F32), pltpu.VMEM((H, V, K), F32), pltpu.VMEM((2, H, V, K), F32),
            pltpu.VMEM((H, 8, K), F32), pltpu.VMEM((H, 8, K), F32),
            dma((5,)), dma((2,)), dma((H, chunks)), dma((H, chunks)), dma((H, chunks)),
            dma((H, chunks)), dma((H, chunks)), dma((H, chunks)),
        ],
        compiler_params=pltpu.CompilerParams(collective_id=0, has_side_effects=True),
    )(queries, keys, values, log_decay, out_grad)
    return pl.pallas_call(
        store_kernel,
        out_shape=tuple(jax.ShapeDtypeStruct(*a) for a in shapes),
        in_specs=[any_spec] * 4,
        out_specs=(any_spec,) * 4,
        scratch_shapes=[dma((4,))],
        compiler_params=pltpu.CompilerParams(vmem_limit_bytes=1 << 20),
    )(*held)


def solution(mesh):
    n_seq = mesh.shape["seq"]
    spec = P(("batch", "seq"), None)
    return jax.shard_map(
        functools.partial(local, n_seq),
        mesh=mesh,
        in_specs=(spec,) * 5,
        out_specs=(spec,) * 4,
        check_vma=False,
    )
```

```python
import functools

import jax
import jax.numpy as jnp
from jax import lax
from jax.experimental import pallas as pl
from jax.experimental.pallas import tpu as pltpu
from jax.sharding import PartitionSpec as P

H = 2
GROUP = 64
ROWS = 64

F32 = jnp.float32
BF16 = jnp.bfloat16


def split(x):
    hi = x.astype(BF16)
    return hi, (x - hi.astype(F32)).astype(BF16)


def mm(a, b):
    return lax.dot_general(a, b, (((1,), (0,)), ((), ())), preferred_element_type=F32)


def mm_nt(a, b):
    return lax.dot_general(a, b, (((1,), (1,)), ((), ())), preferred_element_type=F32)


def mm_tn(a, b):
    return lax.dot_general(a, b, (((0,), (0,)), ((), ())), preferred_element_type=F32)


def three(dot, a, b):
    return dot(a[0], b[0]) + dot(a[0], b[1]) + dot(a[1], b[0])


def kernel(n_seq, L, K, V,
           q_hbm, k_hbm, v_hbm, ld_hbm, do_hbm,
           dq_ref, dk_ref, dv_ref, gd_ref,
           qk_ref, vd_ref, ld_ref,
           acc_q, acc_k, acc_v, rise_ref, tail_ref, whole,
           loc, px, carry, total, relay, ent, ec_own, ec_par,
           in_sem, ec_sem, px_send, px_recv, near_send, near_recv, far_send, far_recv):
    blocks = L // GROUP
    per_head = V // ROWS
    me = lax.axis_index("seq")
    odd = lax.rem(me, 2)
    late = (2 * me >= n_seq).astype(jnp.int32)
    partner = me + 1 - 2 * odd
    up = me + 2 < n_seq
    down = me - 2 >= 0
    sign = (2 * odd - 1, 1 - 2 * odd)
    first = lax.rem(odd + late, 2)
    barrier = pltpu.get_barrier_semaphore()

    def pick(h, x0, x1):
        return jnp.where(h == 0, x0, x1)

    def other_of(h):
        return pick(h, odd, 1 - odd)

    def sign_of(h):
        return pick(h, sign[0], sign[1])

    def reached(device):
        return jnp.logical_and(device >= 0, device < n_seq)

    def has_dst(h):
        return reached(me + 2 * sign_of(h))

    def has_src(h):
        return reached(me - 2 * sign_of(h))

    loads = [
        pltpu.make_async_copy(src, dst, in_sem.at[i])
        for i, (src, dst) in enumerate(
            ((ld_hbm, ld_ref), (k_hbm, qk_ref.at[0]), (q_hbm, qk_ref.at[1]),
             (v_hbm, vd_ref.at[0]), (do_hbm, vd_ref.at[1]))
        )
    ]
    for copy in loads:
        copy.start()

    def tell(device):
        pl.semaphore_signal(barrier, inc=1, device_id={"seq": device},
                            device_id_type=pl.DeviceIdType.MESH)

    tell(partner)

    @pl.when(up)
    def _():
        tell(me + 2)

    @pl.when(down)
    def _():
        tell(me - 2)

    loads[0].wait()
    row = lax.broadcasted_iota(jnp.int32, (L, L), 0)
    col = lax.broadcasted_iota(jnp.int32, (L, L), 1)
    within = jnp.logical_and(row >= col, row // GROUP == col // GROUP)
    tri = jnp.where(within, 1.0, 0.0).astype(BF16)
    ld = ld_ref[...]
    ld0, rest = split(ld)
    mid = ld - ld0.astype(F32)
    low = (mid - rest.astype(F32)).astype(BF16)
    b = mm(tri, ld0) + mm(tri, rest) + mm(tri, low)

    def rows(n):
        return slice(n * GROUP, (n + 1) * GROUP)

    def cols(h):
        return slice(h * K, (h + 1) * K)

    def vcols(h):
        return slice(h * V, (h + 1) * V)

    c = [b[(n + 1) * GROUP - 1:(n + 1) * GROUP, :] for n in range(blocks)]
    before = [jnp.zeros_like(c[0])]
    for n in range(blocks):
        before.append(before[-1] + c[n])
    after = [jnp.zeros_like(c[0])]
    for n in reversed(range(blocks)):
        after.insert(0, after[0] + c[n])
    for n in range(blocks):
        bn = b[rows(n), :]
        rise = jnp.exp(bn)
        tail = jnp.exp(c[n] - bn)
        rise_ref[rows(n), :] = rise
        tail_ref[rows(n), :] = tail
        whole[1, rows(n), :] = rise * jnp.exp(before[n])
        whole[0, rows(n), :] = tail * jnp.exp(after[n + 1])
    gone = jnp.exp(before[blocks])
    for h in range(H):
        ec_own[h] = jnp.broadcast_to(gone[:, cols(h)], (8, K))

    def send(src, dst, ssem, rsem, device):
        return pltpu.make_async_remote_copy(
            src_ref=src, dst_ref=dst, send_sem=ssem, recv_sem=rsem,
            device_id={"seq": device}, device_id_type=pl.DeviceIdType.MESH)

    def part(i):
        return pl.ds(i * ROWS, ROWS)

    def px_copy(h, i):
        r = part(i)
        return send(loc.at[other_of(h), h, r], px.at[h, r], px_send.at[h, i], px_recv.at[h, i], partner)

    def near_copy(h, i):
        r = part(i)
        return send(relay.at[h, r], ent.at[1 - other_of(h), h, r], near_send.at[h, i],
                    near_recv.at[h, i], partner)

    def far_copy(h, i):
        r = part(i)
        return send(total.at[h, r], carry.at[h, r], far_send.at[h, i], far_recv.at[h, i],
                    me + 2 * sign_of(h))

    ec_copy = send(ec_own, ec_par, ec_sem.at[0], ec_sem.at[1], partner)

    for copy in loads[1:]:
        copy.wait()

    def device_total(slot, h):
        kc = pl.ds(pl.multiple_of(h * K, K), K)
        vc = pl.ds(pl.multiple_of(h * V, V), V)
        x = split(qk_ref[slot, :, kc].astype(F32) * whole[slot, :, kc])
        e = mm_tn(vd_ref[slot, :, vc], jnp.concatenate(x, axis=1))
        loc[slot, h] = e[:, :K] + e[:, K:]

    device_total(other_of(first), first)
    pl.semaphore_wait(barrier, 1 + up.astype(jnp.int32) + down.astype(jnp.int32))
    ec_copy.start()
    for i in range(per_head):
        px_copy(first, i).start()
    device_total(other_of(1 - first), 1 - first)
    for i in range(per_head):
        px_copy(1 - first, i).start()
    device_total(1 - other_of(1 - first), 1 - first)
    device_total(1 - other_of(first), first)

    def chain(h, i):
        r = part(i)
        px_copy(h, i).wait_recv()

        @pl.when(has_src(h))
        def _():
            far_copy(h, i).wait_recv()

        mine = 1 - other_of(h)
        came = carry[h, r]
        got = px[h, r]
        own = loc[mine, h, r]

        @pl.when(h == 0)
        def _():
            middle = got + ec_par[h, 0:1, :] * came
            relay[h, r] = came
            ent[mine, h, r] = middle
            total[h, r] = own + ec_own[h, 0:1, :] * middle

        @pl.when(h != 0)
        def _():
            middle = own + ec_own[h, 0:1, :] * came
            relay[h, r] = middle
            ent[mine, h, r] = came
            total[h, r] = got + ec_par[h, 0:1, :] * middle

        @pl.when(has_dst(h))
        def _():
            far_copy(h, i).start()

        @pl.when(jnp.logical_or(h != 0, has_src(h)))
        def _():
            near_copy(h, i).start()

    lead = 1 - first
    for h in range(H):
        @pl.when(jnp.logical_not(has_src(h)))
        def _():
            carry[h] = jnp.zeros((V, K), F32)

    @pl.when(jnp.logical_not(has_src(lead)))
    def _():
        ec_copy.wait_recv()
        for i in range(per_head):
            chain(lead, i)

    for h in range(H):
        k = qk_ref[0, :, cols(h)].astype(F32)
        q = qk_ref[1, :, cols(h)].astype(F32)
        v = vd_ref[0, :, vcols(h)]
        do = vd_ref[1, :, vcols(h)]
        rise = rise_ref[:, cols(h)]
        tail = tail_ref[:, cols(h)]
        bh = b[:, cols(h)]
        k_tail = k * tail
        q_gate = q * rise
        for n in range(blocks):
            width = (n + 1) * GROUP
            keys = [k_tail[rows(m), :] * jnp.exp(sum((c[j][:, cols(h)] for j in range(m + 1, n)),
                                                     jnp.zeros((1, K), F32)))
                    for m in range(n)]
            keys.append(k[rows(n), :] * jnp.exp(-bh[rows(n), :]))
            keys = split(jnp.concatenate(keys, axis=0))
            dots = mm_nt(do[rows(n), :], v[:width, :])
            t = lax.broadcasted_iota(jnp.int32, (GROUP, width), 0) + n * GROUP
            s = lax.broadcasted_iota(jnp.int32, (GROUP, width), 1)
            dots = split(jnp.where(s <= t, dots, 0.0))
            acc_q[rows(n), cols(h)] = rise[rows(n), :] * three(mm, dots, keys)

            length = L - n * GROUP
            tops = [q[rows(n), :] * jnp.exp(bh[rows(n), :] - c[n][:, cols(h)])]
            tops += [q_gate[rows(m), :] * jnp.exp(sum((c[j][:, cols(h)] for j in range(n + 1, m)),
                                                      jnp.zeros((1, K), F32)))
                     for m in range(n + 1, blocks)]
            tops = split(jnp.concatenate(tops, axis=0))
            s = lax.broadcasted_iota(jnp.int32, (GROUP, length), 0)
            t = lax.broadcasted_iota(jnp.int32, (GROUP, length), 1)
            causal = s <= t
            dots = mm_nt(v[rows(n), :], do[n * GROUP:, :])
            dots = split(jnp.where(causal, dots, 0.0))
            acc_k[rows(n), cols(h)] = tail[rows(n), :] * three(mm, dots, tops)
            scores = three(mm_nt, split(k_tail[rows(n), :]), tops)
            scores = split(jnp.where(causal, scores, 0.0))
            acc_v[rows(n), vcols(h)] = mm(scores[0], do[n * GROUP:, :]) + mm(scores[1], do[n * GROUP:, :])

    @pl.when(has_src(lead))
    def _():
        ec_copy.wait_recv()

    lag = (5 * per_head) // 8
    for i in range(per_head + lag):
        if i < per_head:
            @pl.when(has_src(lead))
            def _():
                chain(lead, i)
        if i >= lag:
            chain(1 - lead, i - lag)

    @pl.when(jnp.logical_not(has_dst(0)))
    def _():
        ent[odd, 0] = jnp.zeros((V, K), F32)

    upper = jnp.where(row <= col, 1.0, 0.0).astype(BF16)
    for h in range(H):
        if h == 0:
            @pl.when(has_dst(0))
            def _():
                for i in range(per_head):
                    near_copy(0, i).wait_recv()
        else:
            for i in range(per_head):
                near_copy(h, i).wait_recv()

        start = ent[0, h]
        end = ent[1, h]
        start2 = split(start)
        end2 = split(end)
        a = mm(vd_ref[1, :, vcols(h)], jnp.concatenate(start2, axis=1))
        dq = acc_q[:, cols(h)] + whole[1, :, cols(h)] * (a[:, :K] + a[:, K:])
        a = mm(vd_ref[0, :, vcols(h)], jnp.concatenate(end2, axis=1))
        dk = acc_k[:, cols(h)] + whole[0, :, cols(h)] * (a[:, :K] + a[:, K:])
        ke = split(qk_ref[0, :, cols(h)].astype(F32) * whole[0, :, cols(h)])
        dv = acc_v[:, vcols(h)] + three(mm_nt, ke, end2)
        dq_ref[:, cols(h)] = dq.astype(BF16)
        dk_ref[:, cols(h)] = dk.astype(BF16)
        dv_ref[:, vcols(h)] = dv.astype(BF16)
        leave = ec_own[h, 0:1, :] * start + loc[0, h]
        later = jnp.sum(leave * end, axis=0, keepdims=True)
        terms = split(qk_ref[1, :, cols(h)].astype(F32) * dq - qk_ref[0, :, cols(h)].astype(F32) * dk)
        a = mm(upper, jnp.concatenate(terms, axis=1))
        gd_ref[:, cols(h)] = a[:, :K] + a[:, K:] + later

    ec_copy.wait_send()
    for h in range(H):
        for i in range(per_head):
            px_copy(h, i).wait_send()

        @pl.when(has_dst(h))
        def _():
            for i in range(per_head):
                far_copy(h, i).wait_send()

        if h == 0:
            @pl.when(has_src(0))
            def _():
                for i in range(per_head):
                    near_copy(0, i).wait_send()
        else:
            for i in range(per_head):
                near_copy(h, i).wait_send()


def store_kernel(*refs):
    sems = refs[8]
    copies = [pltpu.make_async_copy(refs[i], refs[4 + i], sems.at[i]) for i in range(4)]
    for copy in copies:
        copy.start()
    for copy in copies:
        copy.wait()


def local(n_seq, queries, keys, values, log_decay, out_grad):
    L, HK = queries.shape
    HV = values.shape[1]
    K, V = HK // H, HV // H
    chunks = V // ROWS
    dma = pltpu.SemaphoreType.DMA
    any_spec = pl.BlockSpec(memory_space=pl.ANY)
    shapes = (((L, HK), BF16), ((L, HK), BF16), ((L, HV), BF16), ((L, HK), F32))
    held = pl.pallas_call(
        functools.partial(kernel, n_seq, L, K, V),
        out_shape=tuple(pltpu.VMEM(*a) for a in shapes),
        in_specs=[any_spec] * 5,
        out_specs=(pl.BlockSpec(memory_space=pltpu.VMEM),) * 4,
        scratch_shapes=[
            pltpu.VMEM((2, L, HK), BF16), pltpu.VMEM((2, L, HV), BF16), pltpu.VMEM((L, HK), F32),
            pltpu.VMEM((L, HK), F32), pltpu.VMEM((L, HK), F32), pltpu.VMEM((L, HV), F32),
            pltpu.VMEM((L, HK), F32), pltpu.VMEM((L, HK), F32), pltpu.VMEM((2, L, HK), F32),
            pltpu.VMEM((2, H, V, K), F32), pltpu.VMEM((H, V, K), F32), pltpu.VMEM((H, V, K), F32),
            pltpu.VMEM((H, V, K), F32), pltpu.VMEM((H, V, K), F32), pltpu.VMEM((2, H, V, K), F32),
            pltpu.VMEM((H, 8, K), F32), pltpu.VMEM((H, 8, K), F32),
            dma((5,)), dma((2,)), dma((H, chunks)), dma((H, chunks)), dma((H, chunks)),
            dma((H, chunks)), dma((H, chunks)), dma((H, chunks)),
        ],
        compiler_params=pltpu.CompilerParams(collective_id=0, has_side_effects=True),
    )(queries, keys, values, log_decay, out_grad)
    return pl.pallas_call(
        store_kernel,
        out_shape=tuple(jax.ShapeDtypeStruct(*a) for a in shapes),
        in_specs=[any_spec] * 4,
        out_specs=(any_spec,) * 4,
        scratch_shapes=[dma((4,))],
        compiler_params=pltpu.CompilerParams(vmem_limit_bytes=1 << 20),
    )(*held)


def solution(mesh):
    n_seq = mesh.shape["seq"]
    spec = P(("batch", "seq"), None)
    return jax.shard_map(
        functools.partial(local, n_seq),
        mesh=mesh,
        in_specs=(spec,) * 5,
        out_specs=(spec,) * 4,
        check_vma=False,
    )
```

```python
import functools

import jax
import jax.numpy as jnp
from jax import lax
from jax.experimental import pallas as pl
from jax.experimental.pallas import tpu as pltpu
from jax.sharding import PartitionSpec as P

H = 2
GROUP = 64
ROWS = 64

F32 = jnp.float32
BF16 = jnp.bfloat16


def split(x):
    hi = x.astype(BF16)
    return hi, (x - hi.astype(F32)).astype(BF16)


def mm(a, b):
    return lax.dot_general(a, b, (((1,), (0,)), ((), ())), preferred_element_type=F32)


def mm_nt(a, b):
    return lax.dot_general(a, b, (((1,), (1,)), ((), ())), preferred_element_type=F32)


def mm_tn(a, b):
    return lax.dot_general(a, b, (((0,), (0,)), ((), ())), preferred_element_type=F32)


def three(dot, a, b):
    return dot(a[0], b[0]) + dot(a[0], b[1]) + dot(a[1], b[0])


def kernel(n_seq, L, K, V,
           q_hbm, k_hbm, v_hbm, ld_hbm, do_hbm,
           dq_ref, dk_ref, dv_ref, gd_ref,
           qk_ref, vd_ref, ld_ref,
           acc_q, acc_k, acc_v, rise_ref, tail_ref, whole,
           loc, px, carry, total, relay, ent, ec_own, ec_par,
           in_sem, ec_sem, px_send, px_recv, near_send, near_recv, far_send, far_recv):
    blocks = L // GROUP
    per_head = V // ROWS
    me = lax.axis_index("seq")
    odd = lax.rem(me, 2)
    late = (2 * me >= n_seq).astype(jnp.int32)
    partner = me + 1 - 2 * odd
    up = me + 2 < n_seq
    down = me - 2 >= 0
    sign = (2 * odd - 1, 1 - 2 * odd)
    first = lax.rem(odd + late, 2)
    barrier = pltpu.get_barrier_semaphore()

    def pick(h, x0, x1):
        return jnp.where(h == 0, x0, x1)

    def other_of(h):
        return pick(h, odd, 1 - odd)

    def sign_of(h):
        return pick(h, sign[0], sign[1])

    def reached(device):
        return jnp.logical_and(device >= 0, device < n_seq)

    def has_dst(h):
        return reached(me + 2 * sign_of(h))

    def has_src(h):
        return reached(me - 2 * sign_of(h))

    loads = [
        pltpu.make_async_copy(src, dst, in_sem.at[i])
        for i, (src, dst) in enumerate(
            ((ld_hbm, ld_ref), (k_hbm, qk_ref.at[0]), (q_hbm, qk_ref.at[1]),
             (v_hbm, vd_ref.at[0]), (do_hbm, vd_ref.at[1]))
        )
    ]
    for copy in loads:
        copy.start()

    def tell(device):
        pl.semaphore_signal(barrier, inc=1, device_id={"seq": device},
                            device_id_type=pl.DeviceIdType.MESH)

    tell(partner)

    @pl.when(up)
    def _():
        tell(me + 2)

    @pl.when(down)
    def _():
        tell(me - 2)

    row = lax.broadcasted_iota(jnp.int32, (L, L), 0)
    col = lax.broadcasted_iota(jnp.int32, (L, L), 1)
    within = jnp.logical_and(row >= col, row // GROUP == col // GROUP)
    tri = jnp.where(within, 1.0, 0.0).astype(BF16)
    loads[0].wait()
    ld = ld_ref[...]
    ld0, rest = split(ld)
    mid = ld - ld0.astype(F32)
    low = (mid - rest.astype(F32)).astype(BF16)
    b = mm(tri, ld0) + mm(tri, rest) + mm(tri, low)

    def rows(n):
        return slice(n * GROUP, (n + 1) * GROUP)

    def cols(h):
        return slice(h * K, (h + 1) * K)

    def vcols(h):
        return slice(h * V, (h + 1) * V)

    c = [b[(n + 1) * GROUP - 1:(n + 1) * GROUP, :] for n in range(blocks)]
    before = [jnp.zeros_like(c[0])]
    for n in range(blocks):
        before.append(before[-1] + c[n])
    after = [jnp.zeros_like(c[0])]
    for n in reversed(range(blocks)):
        after.insert(0, after[0] + c[n])
    for n in range(blocks):
        bn = b[rows(n), :]
        rise = jnp.exp(bn)
        tail = jnp.exp(c[n] - bn)
        rise_ref[rows(n), :] = rise
        tail_ref[rows(n), :] = tail
        whole[1, rows(n), :] = rise * jnp.exp(before[n])
        whole[0, rows(n), :] = tail * jnp.exp(after[n + 1])
    gone = jnp.exp(before[blocks])
    for h in range(H):
        ec_own[h] = jnp.broadcast_to(gone[:, cols(h)], (8, K))

    def send(src, dst, ssem, rsem, device):
        return pltpu.make_async_remote_copy(
            src_ref=src, dst_ref=dst, send_sem=ssem, recv_sem=rsem,
            device_id={"seq": device}, device_id_type=pl.DeviceIdType.MESH)

    def part(i):
        return pl.ds(i * ROWS, ROWS)

    def px_copy(h, i):
        r = part(i)
        return send(loc.at[other_of(h), h, r], px.at[h, r], px_send.at[h, i], px_recv.at[h, i], partner)

    def near_copy(h, i):
        r = part(i)
        return send(relay.at[h, r], ent.at[1 - other_of(h), h, r], near_send.at[h, i],
                    near_recv.at[h, i], partner)

    def far_copy(h, i):
        r = part(i)
        return send(total.at[h, r], carry.at[h, r], far_send.at[h, i], far_recv.at[h, i],
                    me + 2 * sign_of(h))

    ec_copy = send(ec_own, ec_par, ec_sem.at[0], ec_sem.at[1], partner)

    for copy in loads[1:]:
        copy.wait()

    def device_total(slot, h):
        kc = pl.ds(pl.multiple_of(h * K, K), K)
        vc = pl.ds(pl.multiple_of(h * V, V), V)
        x = split(qk_ref[slot, :, kc].astype(F32) * whole[slot, :, kc])
        e = mm_tn(vd_ref[slot, :, vc], jnp.concatenate(x, axis=1))
        loc[slot, h] = e[:, :K] + e[:, K:]

    device_total(other_of(first), first)
    pl.semaphore_wait(barrier, 1 + up.astype(jnp.int32) + down.astype(jnp.int32))
    ec_copy.start()
    for i in range(per_head):
        px_copy(first, i).start()
    device_total(other_of(1 - first), 1 - first)
    for i in range(per_head):
        px_copy(1 - first, i).start()
    device_total(1 - other_of(1 - first), 1 - first)
    device_total(1 - other_of(first), first)

    def chain(h, i):
        r = part(i)
        px_copy(h, i).wait_recv()

        @pl.when(has_src(h))
        def _():
            far_copy(h, i).wait_recv()

        mine = 1 - other_of(h)
        came = carry[h, r]
        got = px[h, r]
        own = loc[mine, h, r]

        def step(static, x1, e1, x2, e2):
            middle = x1 + e1 * came
            total[h, r] = x2 + e2 * middle

            @pl.when(has_dst(h))
            def _():
                far_copy(h, i).start()

            relay[h, r] = middle if static else came
            ent[mine, h, r] = came if static else middle

        @pl.when(h == 0)
        def _():
            step(0, got, ec_par[h, 0:1, :], own, ec_own[h, 0:1, :])

            @pl.when(has_src(h))
            def _():
                near_copy(h, i).start()

        @pl.when(h != 0)
        def _():
            step(1, own, ec_own[h, 0:1, :], got, ec_par[h, 0:1, :])
            near_copy(h, i).start()

    lead = 1 - first
    for h in range(H):
        @pl.when(jnp.logical_not(has_src(h)))
        def _():
            carry[h] = jnp.zeros((V, K), F32)

    @pl.when(jnp.logical_not(has_src(lead)))
    def _():
        ec_copy.wait_recv()
        for i in range(per_head):
            chain(lead, i)

    for h in range(H):
        k = qk_ref[0, :, cols(h)].astype(F32)
        q = qk_ref[1, :, cols(h)].astype(F32)
        v = vd_ref[0, :, vcols(h)]
        do = vd_ref[1, :, vcols(h)]
        rise = rise_ref[:, cols(h)]
        tail = tail_ref[:, cols(h)]
        bh = b[:, cols(h)]
        k_tail = k * tail
        q_gate = q * rise
        for n in range(blocks):
            width = (n + 1) * GROUP
            keys = [k_tail[rows(m), :] * jnp.exp(sum((c[j][:, cols(h)] for j in range(m + 1, n)),
                                                     jnp.zeros((1, K), F32)))
                    for m in range(n)]
            keys.append(k[rows(n), :] * jnp.exp(-bh[rows(n), :]))
            keys = split(jnp.concatenate(keys, axis=0))
            dots = mm_nt(do[rows(n), :], v[:width, :])
            t = lax.broadcasted_iota(jnp.int32, (GROUP, width), 0) + n * GROUP
            s = lax.broadcasted_iota(jnp.int32, (GROUP, width), 1)
            dots = split(jnp.where(s <= t, dots, 0.0))
            acc_q[rows(n), cols(h)] = rise[rows(n), :] * three(mm, dots, keys)

            length = L - n * GROUP
            tops = [q[rows(n), :] * jnp.exp(bh[rows(n), :] - c[n][:, cols(h)])]
            tops += [q_gate[rows(m), :] * jnp.exp(sum((c[j][:, cols(h)] for j in range(n + 1, m)),
                                                      jnp.zeros((1, K), F32)))
                     for m in range(n + 1, blocks)]
            tops = split(jnp.concatenate(tops, axis=0))
            s = lax.broadcasted_iota(jnp.int32, (GROUP, length), 0)
            t = lax.broadcasted_iota(jnp.int32, (GROUP, length), 1)
            causal = s <= t
            dots = mm_nt(v[rows(n), :], do[n * GROUP:, :])
            dots = split(jnp.where(causal, dots, 0.0))
            acc_k[rows(n), cols(h)] = tail[rows(n), :] * three(mm, dots, tops)
            scores = three(mm_nt, split(k_tail[rows(n), :]), tops)
            scores = split(jnp.where(causal, scores, 0.0))
            acc_v[rows(n), vcols(h)] = mm(scores[0], do[n * GROUP:, :]) + mm(scores[1], do[n * GROUP:, :])

    @pl.when(has_src(lead))
    def _():
        ec_copy.wait_recv()

    lag = 3
    for i in range(per_head + lag):
        if i < per_head:
            @pl.when(has_src(lead))
            def _():
                chain(lead, i)
        if i >= lag:
            chain(1 - lead, i - lag)

    @pl.when(jnp.logical_not(has_dst(0)))
    def _():
        ent[odd, 0] = jnp.zeros((V, K), F32)

    upper = jnp.where(row <= col, 1.0, 0.0).astype(BF16)
    for h in range(H):
        if h == 0:
            @pl.when(has_dst(0))
            def _():
                for i in range(per_head):
                    near_copy(0, i).wait_recv()
        else:
            for i in range(per_head):
                near_copy(h, i).wait_recv()

        start = ent[0, h]
        end = ent[1, h]
        start2 = split(start)
        end2 = split(end)
        a = mm(vd_ref[1, :, vcols(h)], jnp.concatenate(start2, axis=1))
        dq = acc_q[:, cols(h)] + whole[1, :, cols(h)] * (a[:, :K] + a[:, K:])
        a = mm(vd_ref[0, :, vcols(h)], jnp.concatenate(end2, axis=1))
        dk = acc_k[:, cols(h)] + whole[0, :, cols(h)] * (a[:, :K] + a[:, K:])
        ke = split(qk_ref[0, :, cols(h)].astype(F32) * whole[0, :, cols(h)])
        dv = acc_v[:, vcols(h)] + three(mm_nt, ke, end2)
        dq_ref[:, cols(h)] = dq.astype(BF16)
        dk_ref[:, cols(h)] = dk.astype(BF16)
        dv_ref[:, vcols(h)] = dv.astype(BF16)
        leave = ec_own[h, 0:1, :] * start + loc[0, h]
        later = jnp.sum(leave * end, axis=0, keepdims=True)
        terms = split(qk_ref[1, :, cols(h)].astype(F32) * dq - qk_ref[0, :, cols(h)].astype(F32) * dk)
        a = mm(upper, jnp.concatenate(terms, axis=1))
        gd_ref[:, cols(h)] = a[:, :K] + a[:, K:] + later

    ec_copy.wait_send()
    for h in range(H):
        for i in range(per_head):
            px_copy(h, i).wait_send()

        @pl.when(has_dst(h))
        def _():
            for i in range(per_head):
                far_copy(h, i).wait_send()

        if h == 0:
            @pl.when(has_src(0))
            def _():
                for i in range(per_head):
                    near_copy(0, i).wait_send()
        else:
            for i in range(per_head):
                near_copy(h, i).wait_send()


def store_kernel(*refs):
    sems = refs[8]
    copies = [pltpu.make_async_copy(refs[i], refs[4 + i], sems.at[i]) for i in range(4)]
    for copy in copies:
        copy.start()
    for copy in copies:
        copy.wait()


def local(n_seq, queries, keys, values, log_decay, out_grad):
    L, HK = queries.shape
    HV = values.shape[1]
    K, V = HK // H, HV // H
    chunks = V // ROWS
    dma = pltpu.SemaphoreType.DMA
    any_spec = pl.BlockSpec(memory_space=pl.ANY)
    shapes = (((L, HK), BF16), ((L, HK), BF16), ((L, HV), BF16), ((L, HK), F32))
    held = pl.pallas_call(
        functools.partial(kernel, n_seq, L, K, V),
        out_shape=tuple(pltpu.VMEM(*a) for a in shapes),
        in_specs=[any_spec] * 5,
        out_specs=(pl.BlockSpec(memory_space=pltpu.VMEM),) * 4,
        scratch_shapes=[
            pltpu.VMEM((2, L, HK), BF16), pltpu.VMEM((2, L, HV), BF16), pltpu.VMEM((L, HK), F32),
            pltpu.VMEM((L, HK), F32), pltpu.VMEM((L, HK), F32), pltpu.VMEM((L, HV), F32),
            pltpu.VMEM((L, HK), F32), pltpu.VMEM((L, HK), F32), pltpu.VMEM((2, L, HK), F32),
            pltpu.VMEM((2, H, V, K), F32), pltpu.VMEM((H, V, K), F32), pltpu.VMEM((H, V, K), F32),
            pltpu.VMEM((H, V, K), F32), pltpu.VMEM((H, V, K), F32), pltpu.VMEM((2, H, V, K), F32),
            pltpu.VMEM((H, 8, K), F32), pltpu.VMEM((H, 8, K), F32),
            dma((5,)), dma((2,)), dma((H, chunks)), dma((H, chunks)), dma((H, chunks)),
            dma((H, chunks)), dma((H, chunks)), dma((H, chunks)),
        ],
        compiler_params=pltpu.CompilerParams(collective_id=0, has_side_effects=True),
    )(queries, keys, values, log_decay, out_grad)
    return pl.pallas_call(
        store_kernel,
        out_shape=tuple(jax.ShapeDtypeStruct(*a) for a in shapes),
        in_specs=[any_spec] * 4,
        out_specs=(any_spec,) * 4,
        scratch_shapes=[dma((4,))],
        compiler_params=pltpu.CompilerParams(vmem_limit_bytes=1 << 20),
    )(*held)


def solution(mesh):
    n_seq = mesh.shape["seq"]
    spec = P(("batch", "seq"), None)
    return jax.shard_map(
        functools.partial(local, n_seq),
        mesh=mesh,
        in_specs=(spec,) * 5,
        out_specs=(spec,) * 4,
        check_vma=False,
    )
```
